1024 devices in a mesh: owner: 64 (over x, z), rep: 16 (over y, core).
Axes of the slice: x: 4, y: 8, z: 16, core: 2. Of those that a mesh axis runs over, the one named last changes fastest.
Arguments:
- stay_rows: bfloat16 [512, 1024, 1024], P('owner', 'rep'), may hold values from -40 to 40
- stay_count: int32 [512, 16], P('owner', 'rep'), may hold values from 1 to 64, as said below
- moving_rows: bfloat16 [524288, 1024], P(('owner', 'rep')), may hold values from -5 to 5
- new_list: int32 [524288], P(('owner', 'rep')), may hold values from 0 to 511, as said below
- centroids: bfloat16 [512, 128, 1024], P('owner'), may hold values from -2 to 2
- sharpness: float32 [512], P('owner'), may hold values from 0.5 to 2
Outputs:
- refreshed: bfloat16 [512, 128, 1024], P('owner')
- mass: float32 [512, 128], P('owner', 'rep')
The draws below stay inside these ranges and needn't reach their ends.
Inputs may be any that keep to these rules, and one draw needn't show every extreme that they name: `stay_count`: slots 0 to count - 1 of a list on a replica are live; some entry equals 64. `new_list`: within the rows of one device, each list is named at most 2 times, and on every device some list is named exactly 2 times.
All inputs are finite; a program needn't handle non-finite values.
Results may differ from the reference program's by a relative error of at most 0.0032.
Values may be sent and summed in bfloat16 or wider, within the bound.
No kernel may reach another device: no remote copies, remote signals or barrier semaphores. Data moves between devices by JAX's collectives and lax.ppermute only.
A program may use at most 64 MiB of HBM per device.

```python
import math
import jax
import jax.numpy as jnp
from jax import lax

D = 1024
F = 128
LIST_DEV = 8
CAP = 64
SLOT_L = 2
LISTS = 512
OUT_DEV = 512
MOVING = 524288
N_OWNER = 64
N_REP = 16


def centre_table(key):
    table = 0.5 * jax.random.normal(jax.random.fold_in(key, 11), (LISTS, F, D), jnp.float32)
    return jnp.clip(table, -2.0, 2.0)


def draw_centroids(key, part):
    return centre_table(key).astype(jnp.bfloat16)


def draw_stay_rows(key, part):
    values = jnp.clip(jax.random.normal(jax.random.fold_in(key, 13), (LISTS, N_REP * CAP, D), jnp.float32), -4.0, 4.0)
    return values.astype(jnp.bfloat16)


def draw_stay_count(key, part):
    base_key = jax.random.fold_in(key, 3)
    device_shift = jax.random.randint(jax.random.fold_in(base_key, 1), (LISTS // LIST_DEV, N_REP), 0, 3)
    shift_amount = jnp.repeat(device_shift, LIST_DEV, axis=0) + jax.random.randint(jax.random.fold_in(base_key, 2), (LISTS, N_REP), 0, 2)
    top_count = jnp.maximum(jnp.right_shift(jnp.full((LISTS, N_REP), CAP, jnp.int32), shift_amount.astype(jnp.int32)), 1)
    counts = 1 + jax.random.randint(jax.random.fold_in(base_key, 3), (LISTS, N_REP), 0, top_count)
    return counts.at[0, 0].set(CAP).astype(jnp.int32)


def route_targets(key):
    device_total = MOVING // OUT_DEV
    slot_total = LISTS * SLOT_L
    device_keys = jax.random.split(jax.random.fold_in(key, 5), device_total)

    def one_device(device_key):
        first_key = jax.random.fold_in(device_key, 1)
        second_key = jax.random.fold_in(device_key, 2)
        shuffled = jax.random.permutation(first_key, slot_total)
        chosen_list = shuffled[0] // SLOT_L
        order_key = jnp.where(shuffled // SLOT_L == chosen_list, slot_total + jnp.arange(slot_total), jnp.arange(slot_total))
        remaining = shuffled[jnp.argsort(order_key, stable=True)]
        picked = jnp.concatenate([chosen_list * SLOT_L + jnp.arange(SLOT_L), remaining[:OUT_DEV - SLOT_L]])
        return picked[jax.random.permutation(second_key, OUT_DEV)]
    return jax.vmap(one_device)(device_keys).reshape(-1).astype(jnp.int32)


def draw_new_list(key, part):
    return (route_targets(key) // SLOT_L).astype(jnp.int32)


def level_of(stream_key, shape, shards, smallest, largest):
    def one(position, blocks):
        heights = jax.random.uniform(jax.random.fold_in(jax.random.fold_in(stream_key, 6), position), (blocks,), jnp.float32, smallest / len(shards), largest / len(shards))
        return jnp.repeat(jnp.exp(heights), shape[position] // blocks).reshape((-1,) + (1,) * (len(shape) - position - 1))

    factor_of = one(*shards[0])
    for cut in shards[1:]:
        factor_of = factor_of * one(*cut)
    return factor_of


def gaussian(own_key, shape, width, bound, cuts=(), held_as=jnp.bfloat16):
    gain = level_of(own_key, shape, cuts, -0.22, 0.18) if cuts else 1.0
    entries = jax.random.normal(own_key, shape, jnp.float32) * width * gain
    return jnp.minimum(jnp.maximum(entries, -bound), bound).astype(held_as)


def setup_inputs(seed: int = 0) -> dict:
    keys = jax.random.split(jax.random.key(seed), 7)
    return {
        "stay_rows": draw_stay_rows(jax.random.fold_in(keys[6], 71), 0),
        "stay_count": draw_stay_count(jax.random.fold_in(keys[6], 71), 0),
        "moving_rows": gaussian(keys[2], (MOVING, D), 1.0, 5.0, ((0, 1024),)),
        "new_list": draw_new_list(jax.random.fold_in(keys[6], 71), 0),
        "centroids": draw_centroids(jax.random.fold_in(keys[6], 71), 0),
        "sharpness": jnp.clip(jnp.exp(math.log(2.0) - 1.3862944 * jax.random.uniform(keys[5], (LISTS,), jnp.float32) ** level_of(keys[5], (LISTS,), ((0, 64),), -0.2, 0.2)), 0.5, 2.0),
    }


prior_weight = 1.0

def soft_stats(members, live_mask, centres, sharp):
    products = jnp.dot(members, centres.T, preferred_element_type=jnp.float32)
    centre_norm = lax.optimization_barrier(jnp.sum(jnp.square(centres.astype(jnp.float32)), axis=-1))
    scores = sharp * (2.0 * products - centre_norm[None, :]) / math.sqrt(D)
    weights = jax.nn.softmax(scores, axis=-1).astype(jnp.bfloat16) * live_mask[:, None].astype(jnp.bfloat16)
    numerator = jnp.dot(weights.T, members, preferred_element_type=jnp.float32)
    mass_sum = lax.optimization_barrier(jnp.sum(weights.astype(jnp.float32), axis=0))
    return (numerator, mass_sum)

def reference(stay_rows, stay_count, moving_rows, new_list, centroids, sharpness):
    limit = N_OWNER * N_REP * SLOT_L
    order = jnp.argsort(new_list, stable=True)
    arrived_sorted = jnp.concatenate([moving_rows[order], jnp.zeros((limit, D), moving_rows.dtype)], axis=0)
    arrive_count = jnp.zeros((LISTS,), jnp.int32).at[new_list].add(1).astype(jnp.int32)
    arrive_start = (jnp.cumsum(arrive_count) - arrive_count).astype(jnp.int32)

    def one_list(items):
        members, live_count, centres, sharp, offset, count = items
        stay_mask = (jnp.arange(CAP)[None, :] < live_count[:, None]).reshape(-1)
        first_num, first_mass = soft_stats(members, stay_mask, centres, sharp)
        arrivals = lax.dynamic_slice_in_dim(arrived_sorted, offset.astype(jnp.int32), limit, 0)
        arrive_mask = jnp.arange(limit) < count
        second_num, second_mass = soft_stats(arrivals, arrive_mask, centres, sharp)
        numerator = first_num + second_num
        mass_sum = first_mass + second_mass
        refreshed = ((numerator + prior_weight * centres.astype(jnp.float32)) / (mass_sum[:, None] + prior_weight)).astype(jnp.bfloat16)
        return (refreshed, mass_sum)
    refreshed, mass = lax.map(one_list, (stay_rows, stay_count, centroids, sharpness, arrive_start, arrive_count))
    return (refreshed, mass)
```

```python
import functools
import math

import jax
import jax.numpy as jnp
from jax import lax
from jax.experimental import pallas as pl
from jax.experimental.pallas import tpu as pltpu
from jax.sharding import Mesh
from jax.sharding import PartitionSpec as P

SLOT_L = 2
EMPTY = 1024.0
LIMIT = 512.0
LANES = 128
NOTE = 16
ROOM = 24 * 1024 * 1024


def shifted(n, by):
    return [(i, (i + by) % n) for i in range(n)]


def pack_kernel(position_ref, rows_ref, out_ref):
    block, slots, features = out_ref.shape
    rows = block * slots
    count = rows_ref.shape[0]
    here = lax.broadcasted_iota(jnp.int32, (rows, count), 0) + pl.program_id(0) * rows
    hit = here == position_ref[...]
    pick = jnp.where(hit, 1.0, 0.0)
    held = jnp.sum(pick, axis=1, keepdims=True)
    out = jnp.dot(pick.astype(jnp.bfloat16), rows_ref[...], preferred_element_type=jnp.float32)
    lane = lax.broadcasted_iota(jnp.int32, (rows, features), 1)
    out = jnp.where((lane == 0) & (held < 0.5), EMPTY, out)
    out_ref[...] = out.astype(jnp.bfloat16).reshape(block, slots, features)


def pack(moving_rows, new_list, lists):
    count, features = moving_rows.shape
    order = jnp.arange(count)
    earlier = (new_list[:, None] == new_list[None, :]) & (order[:, None] < order[None, :])
    position = new_list * SLOT_L + jnp.sum(earlier.astype(jnp.int32), axis=0)
    steps = 4
    return pl.pallas_call(
        pack_kernel,
        out_shape=jax.ShapeDtypeStruct((lists, SLOT_L, features), jnp.bfloat16),
        grid=(steps,),
        in_specs=[
            pl.BlockSpec((1, count), lambda i: (0, 0)),
            pl.BlockSpec((count, features), lambda i: (0, 0)),
        ],
        out_specs=pl.BlockSpec((lists // steps, SLOT_L, features), lambda i: (i, 0, 0)),
        name="pack",
    )(position[None, :], moving_rows)


def weigh_block(members, centres, norm, sharp):
    features = members.shape[1]
    products = lax.dot_general(
        members, centres, (((1,), (1,)), ((), ())), preferred_element_type=jnp.float32
    )
    scores = sharp * (2.0 * products - norm) / math.sqrt(features)
    powers = jnp.exp(scores - jnp.max(scores, axis=1, keepdims=True))
    weights = powers / jnp.sum(powers, axis=1, keepdims=True)
    live = members[:, 0:1].astype(jnp.float32) < LIMIT
    weights = jnp.where(live, weights, 0.0).astype(jnp.bfloat16)
    down = (((0,), (0,)), ((), ()))
    numerator = lax.dot_general(weights, members, down, preferred_element_type=jnp.float32)
    ones = jnp.ones((members.shape[0], LANES), jnp.bfloat16)
    mass = lax.dot_general(weights, ones, down, preferred_element_type=jnp.float32)
    return numerator, mass


def stay_kernel(sharp_ref, members_ref, centres_ref, norm_ref, out_ref):
    features = centres_ref.shape[1]
    numerator, mass = weigh_block(members_ref[...], centres_ref[...], norm_ref[...], sharp_ref[0])

    @pl.when(pl.program_id(0) == 0)
    def _():
        out_ref[...] = jnp.zeros_like(out_ref)

    out_ref[:, :features] += numerator
    out_ref[:, features:] += mass


def stay_sums(members, centres, norm, sharp):
    rows, features = members.shape
    fines = centres.shape[0]
    steps = 2
    return pl.pallas_call(
        stay_kernel,
        out_shape=jax.ShapeDtypeStruct((fines, features + LANES), jnp.float32),
        grid=(steps,),
        in_specs=[
            pl.BlockSpec(memory_space=pltpu.SMEM),
            pl.BlockSpec((rows // steps, features), lambda i: (i, 0)),
            pl.BlockSpec((fines, features), lambda i: (0, 0)),
            pl.BlockSpec((1, fines), lambda i: (0, 0)),
        ],
        out_specs=pl.BlockSpec((fines, features + LANES), lambda i: (0, 0)),
        name="stay_sums",
        compiler_params=pltpu.CompilerParams(vmem_limit_bytes=ROOM),
    )(sharp, members, centres, norm)


def move_kernel(
    sharp_ref, core_ref, members_ref, centres_ref, norm_ref, before_ref, mine_ref, theirs_ref, sums
):
    features = centres_ref.shape[1]
    half = mine_ref.shape[0]
    members = members_ref[...].reshape(-1, features)
    numerator, mass = weigh_block(members, centres_ref[...], norm_ref[...], sharp_ref[0])

    @pl.when(pl.program_id(0) == 0)
    def _():
        sums[...] = before_ref[...]

    sums[:, :features] += numerator
    sums[:, features:] += mass

    @pl.when(pl.program_id(0) == pl.num_programs(0) - 1)
    def _():
        core = core_ref[0]
        mine_ref[...] = sums[pl.ds(pl.multiple_of(core * half, half), half), :]
        theirs_ref[...] = sums[pl.ds(pl.multiple_of((1 - core) * half, half), half), :]


def move_sums(arrived, centres, norm, sharp, before, core):
    sources, slots, features = arrived.shape
    fines = centres.shape[0]
    half = fines // 2
    steps = 4
    wide = features + LANES
    part = jax.ShapeDtypeStruct((half, wide), jnp.float32)
    return pl.pallas_call(
        move_kernel,
        out_shape=(part, part),
        grid=(steps,),
        in_specs=[
            pl.BlockSpec(memory_space=pltpu.SMEM),
            pl.BlockSpec(memory_space=pltpu.SMEM),
            pl.BlockSpec((sources // steps, slots, features), lambda i: (i, 0, 0)),
            pl.BlockSpec((fines, features), lambda i: (0, 0)),
            pl.BlockSpec((1, fines), lambda i: (0, 0)),
            pl.BlockSpec((fines, wide), lambda i: (0, 0)),
        ],
        out_specs=[pl.BlockSpec((half, wide), lambda i: (0, 0))] * 2,
        scratch_shapes=[pltpu.VMEM((fines, wide), jnp.float32)],
        name="move_sums",
        compiler_params=pltpu.CompilerParams(vmem_limit_bytes=ROOM),
    )(sharp, core, arrived, centres, norm, before)


def refresh_kernel(core_ref, mine_ref, other_ref, centres_ref, out_ref):
    copies, _, _ = out_ref.shape
    half, wide = mine_ref.shape
    features = wide - LANES
    total = mine_ref[...] + other_ref[...]
    mass = total[:, features:]
    core = core_ref[0]
    own = centres_ref[pl.ds(pl.multiple_of(core * half, half), half), :].astype(jnp.float32)
    scale = mass + 1.0
    for j in range(features // LANES):
        span = slice(j * LANES, (j + 1) * LANES)
        block = ((total[:, span] + own[:, span]) / scale).astype(jnp.bfloat16)
        for i in range(half // NOTE):
            at = (i * (features // LANES) + j) * NOTE
            piece = block[i * NOTE : (i + 1) * NOTE]
            for k in range(copies):
                out_ref[k, at : at + NOTE, :] = piece
    row = lax.broadcasted_iota(jnp.int32, (half, LANES), 0)
    lane = lax.broadcasted_iota(jnp.int32, (half, LANES), 1)
    flat = jnp.sum(jnp.where(row == lane, mass, 0.0), axis=0, keepdims=True)
    high = flat.astype(jnp.bfloat16).astype(jnp.float32)
    middle = (flat - high).astype(jnp.bfloat16).astype(jnp.float32)
    low = flat - high - middle
    line = lax.broadcasted_iota(jnp.int32, (NOTE, LANES), 0)
    note = jnp.where(line == 0, high, jnp.where(line == 1, middle, jnp.where(line == 2, low, 0.0)))
    note = note.astype(jnp.bfloat16)
    for k in range(copies):
        out_ref[k, half * features // LANES :, :] = note


def refresh(mine, other, centres, core, copies):
    half, wide = mine.shape
    fines, features = centres.shape
    whole = lambda *shape: pl.BlockSpec(shape, lambda: (0,) * len(shape))
    lines = half * features // LANES + NOTE
    return pl.pallas_call(
        refresh_kernel,
        out_shape=jax.ShapeDtypeStruct((copies, lines, LANES), jnp.bfloat16),
        in_specs=[
            pl.BlockSpec(memory_space=pltpu.SMEM),
            whole(half, wide),
            whole(half, wide),
            whole(fines, features),
        ],
        out_specs=whole(copies, lines, LANES),
        name="refresh",
        compiler_params=pltpu.CompilerParams(vmem_limit_bytes=ROOM),
    )(core, mine, other, centres)


def assemble_kernel(place_ref, near_ref, far_ref, out_ref, mass_ref):
    lists, share = mass_ref.shape
    _, fines, features = out_ref.shape
    half = fines // 2
    core, holder, offset = place_ref[0], place_ref[1], place_ref[2]
    step = pl.program_id(0)
    for ref, at in ((near_ref, core), (far_ref, 1 - core)):
        for j in range(features // LANES):
            for i in range(half // NOTE):
                line = (i * (features // LANES) + j) * NOTE
                start = pl.multiple_of(at * half + i * NOTE, NOTE)
                out_ref[0, pl.ds(start, NOTE), j * LANES : (j + 1) * LANES] = ref[
                    0, line : line + NOTE, :
                ]
    notes = half * features // LANES

    def mass_of(ref):
        note = ref[0, notes:, :].astype(jnp.float32)
        return (note[0:1] + note[1:2]) + note[2:3]

    mass = jnp.where(holder == core, mass_of(near_ref), mass_of(far_ref))
    row = lax.broadcasted_iota(jnp.int32, (share, LANES), 0)
    lane = lax.broadcasted_iota(jnp.int32, (share, LANES), 1)
    column = lax.broadcasted_iota(jnp.int32, (lists, share), 1)
    line = lax.broadcasted_iota(jnp.int32, (lists, share), 0)
    result = jnp.zeros((lists, share), jnp.float32)
    for k in range(share):
        value = jnp.sum(jnp.where(lane[0:1] == offset + k, mass, 0.0))
        result = jnp.where(column == k, value, result)

    @pl.when(step == 0)
    def _():
        mass_ref[...] = result

    mass_ref[...] = jnp.where(line == step, result, mass_ref[...])


def assemble(near, far, place, fines, features, share):
    lists, lines, _ = near.shape
    return pl.pallas_call(
        assemble_kernel,
        out_shape=(
            jax.ShapeDtypeStruct((lists, fines, features), jnp.bfloat16),
            jax.ShapeDtypeStruct((lists, share), jnp.float32),
        ),
        grid=(lists,),
        in_specs=[
            pl.BlockSpec(memory_space=pltpu.SMEM),
            pl.BlockSpec((1, lines, LANES), lambda i: (i, 0, 0)),
            pl.BlockSpec((1, lines, LANES), lambda i: (i, 0, 0)),
        ],
        out_specs=[
            pl.BlockSpec((1, fines, features), lambda i: (i, 0, 0)),
            pl.BlockSpec((lists, share), lambda i: (0, 0)),
        ],
        name="assemble",
        compiler_params=pltpu.CompilerParams(vmem_limit_bytes=ROOM),
    )(place, near, far)


def local(stay_rows, stay_count, moving_rows, new_list, centroids, sharpness):
    owners, columns, cores = (lax.axis_size(a) for a in ("owner", "y", "core"))
    lists_here, capacity, features = stay_rows.shape
    fine_count = centroids.shape[1]
    half = fine_count // cores
    share = fine_count // (columns * cores)
    y = lax.axis_index("y")
    core = lax.axis_index("core")

    outgoing = pack(moving_rows, new_list, owners * lists_here)
    arrived = lax.all_to_all(outgoing, ("owner", "y"), split_axis=0, concat_axis=0, tiled=True)

    dead = jnp.arange(capacity)[None, :, None] >= stay_count[:, :, None]
    first = jnp.arange(features)[None, None, :] == 0
    stay = jnp.where(dead & first, jnp.bfloat16(EMPTY), stay_rows)
    residents = []
    for by in range(columns):
        block = lax.dynamic_index_in_dim(stay, (y + by) & (columns - 1), 0, keepdims=False)
        residents.append(lax.ppermute(block, "y", shifted(columns, by)) if by else block)
    residents = jnp.concatenate(residents, axis=0)

    centres = lax.dynamic_index_in_dim(centroids, y, 0, keepdims=False)
    sharp = lax.dynamic_slice_in_dim(sharpness, y, 1, 0)
    norm = jnp.sum(jnp.square(centres.astype(jnp.float32)), axis=-1)[None, :]
    place = core.astype(jnp.int32)[None]
    before = stay_sums(residents, centres, norm, sharp)
    mine, theirs = move_sums(arrived, centres, norm, sharp, before, place)
    other = lax.ppermute(theirs, "core", shifted(cores, 1))
    copies = refresh(mine, other, centres, place, columns)
    near = lax.all_to_all(copies, "y", split_axis=0, concat_axis=0, tiled=True)
    far = lax.ppermute(near, "core", shifted(cores, 1))
    start = (y * cores + core) * share
    place = jnp.stack([core, start // half, start % half]).astype(jnp.int32)
    return assemble(near, far, place, fine_count, features, share)


def solution(mesh):
    split = Mesh(mesh.devices.reshape(mesh.devices.shape[0], -1, 2), ("owner", "y", "core"))
    rep = ("y", "core")
    in_specs = (
        P("owner", rep, None),
        P("owner", rep),
        P(("owner", "y", "core"), None),
        P(("owner", "y", "core")),
        P("owner", None, None),
        P("owner"),
    )
    out_specs = (P("owner", None, None), P("owner", rep))
    return jax.shard_map(
        local, mesh=split, in_specs=in_specs, out_specs=out_specs, check_vma=False
    )
```

```python
import math

import jax
import jax.numpy as jnp
from jax import lax
from jax.experimental import pallas as pl
from jax.experimental.pallas import tpu as pltpu
from jax.sharding import Mesh
from jax.sharding import PartitionSpec as P

SLOT_L = 2
EMPTY = 1024.0
LIMIT = 512.0
LANES = 128
NOTE = 16
ROOM = 24 * 1024 * 1024


def shifted(n, by):
    return [(i, (i + by) % n) for i in range(n)]


def pack_kernel(list_ref, rows_hbm, out_ref, rows, position, sem):
    block, slots, features = out_ref.shape
    many = block * slots
    count = rows.shape[0]
    fetch = pltpu.make_async_copy(rows_hbm, rows, sem)

    @pl.when(pl.program_id(0) == 0)
    def _():
        fetch.start()
        across = jnp.broadcast_to(list_ref[...], (count, count))
        down = jnp.transpose(across)
        row = lax.broadcasted_iota(jnp.int32, (count, count), 0)
        column = lax.broadcasted_iota(jnp.int32, (count, count), 1)
        earlier = jnp.where((across == down) & (row < column), 1.0, 0.0)
        slot = jnp.sum(earlier, axis=0, keepdims=True).astype(jnp.int32)
        position[...] = list_ref[...] * slots + slot
        fetch.wait()

    here = lax.broadcasted_iota(jnp.int32, (many, count), 0) + pl.program_id(0) * many
    pick = jnp.where(here == position[...], 1.0, 0.0)
    held = jnp.sum(pick, axis=1, keepdims=True)
    out = jnp.dot(pick.astype(jnp.bfloat16), rows[...], preferred_element_type=jnp.float32)
    lane = lax.broadcasted_iota(jnp.int32, (many, features), 1)
    out = jnp.where((lane == 0) & (held < 0.5), EMPTY, out)
    out_ref[...] = out.astype(jnp.bfloat16).reshape(block, slots, features)


def pack(moving_rows, new_list, lists):
    count, features = moving_rows.shape
    steps = 4
    return pl.pallas_call(
        pack_kernel,
        out_shape=jax.ShapeDtypeStruct((lists, SLOT_L, features), jnp.bfloat16),
        grid=(steps,),
        in_specs=[
            pl.BlockSpec((1, count), lambda i: (0, 0)),
            pl.BlockSpec(memory_space=pl.ANY),
        ],
        out_specs=pl.BlockSpec((lists // steps, SLOT_L, features), lambda i: (i, 0, 0)),
        scratch_shapes=[
            pltpu.VMEM((count, features), jnp.bfloat16),
            pltpu.VMEM((1, count), jnp.int32),
            pltpu.SemaphoreType.DMA,
        ],
        name="pack",
    )(new_list[None, :], moving_rows)


DOWN = (((0,), (0,)), ((), ()))


def weights_of(members, centres, norm, sharp):
    features = members.shape[1]
    products = lax.dot_general(
        members, centres, (((1,), (1,)), ((), ())), preferred_element_type=jnp.float32
    )
    scores = sharp * (2.0 * products - norm) / math.sqrt(features)
    powers = jnp.exp(scores - jnp.max(scores, axis=1, keepdims=True))
    total = jnp.sum(powers, axis=1, keepdims=True)
    largest = jnp.max(members[:, :LANES].astype(jnp.float32), axis=1, keepdims=True)
    return (powers * jnp.where(largest < LIMIT, 1.0 / total, 0.0)).astype(jnp.bfloat16)


def weigh_block(members, centres, norm, sharp):
    weights = weights_of(members, centres, norm, sharp)
    numerator = lax.dot_general(weights, members, DOWN, preferred_element_type=jnp.float32)
    ones = jnp.ones((members.shape[0], LANES), jnp.bfloat16)
    mass = lax.dot_general(weights, ones, DOWN, preferred_element_type=jnp.float32)
    return numerator, mass


def stay_kernel(sharp_ref, members_ref, centres_ref, norm_ref, out_ref):
    features = centres_ref.shape[1]
    numerator, mass = weigh_block(members_ref[...], centres_ref[...], norm_ref[...], sharp_ref[0])

    @pl.when(pl.program_id(0) == 0)
    def _():
        out_ref[...] = jnp.zeros_like(out_ref)

    out_ref[:, :features] += numerator
    out_ref[:, features:] += mass


def stay_sums(members, centres, norm, sharp):
    rows, features = members.shape
    fines = centres.shape[0]
    steps = 2
    return pl.pallas_call(
        stay_kernel,
        out_shape=jax.ShapeDtypeStruct((fines, features + LANES), jnp.float32),
        grid=(steps,),
        in_specs=[
            pl.BlockSpec(memory_space=pltpu.SMEM),
            pl.BlockSpec((rows // steps, features), lambda i: (i, 0)),
            pl.BlockSpec((fines, features), lambda i: (0, 0)),
            pl.BlockSpec((1, fines), lambda i: (0, 0)),
        ],
        out_specs=pl.BlockSpec((fines, features + LANES), lambda i: (0, 0)),
        name="stay_sums",
        compiler_params=pltpu.CompilerParams(vmem_limit_bytes=ROOM),
    )(sharp, members, centres, norm)


def move_kernel(
    sharp_ref, core_ref, members_ref, centres_ref, norm_ref, before_ref, mine_ref, theirs_ref,
    members, weights,
):
    rows, features = members.shape
    half = mine_ref.shape[0]
    steps = 4
    block = rows // steps
    for i in range(steps):
        span = slice(i * block, (i + 1) * block)
        sources = slice(i * block // SLOT_L, (i + 1) * block // SLOT_L)
        part = members_ref[sources].reshape(block, features)
        members[span] = part
        weights[span] = weights_of(part, centres_ref[...], norm_ref[...], sharp_ref[0])

    first = core_ref[0] == 0

    def split(at, value):
        value = value + before_ref[:, at]
        mine_ref[:, at] = jnp.where(first, value[:half], value[half:])
        theirs_ref[:, at] = jnp.where(first, value[half:], value[:half])

    wide = 2 * LANES
    for j in range(features // wide):
        at = slice(j * wide, (j + 1) * wide)
        split(
            at,
            lax.dot_general(
                weights[...], members[:, at], DOWN, preferred_element_type=jnp.float32
            ),
        )
    ones = jnp.ones((rows, LANES), jnp.bfloat16)
    split(
        slice(features, features + LANES),
        lax.dot_general(weights[...], ones, DOWN, preferred_element_type=jnp.float32),
    )


def move_sums(arrived, centres, norm, sharp, before, core):
    sources, slots, features = arrived.shape
    fines = centres.shape[0]
    part = jax.ShapeDtypeStruct((fines // 2, features + LANES), jnp.float32)
    vmem = pl.BlockSpec(memory_space=pltpu.VMEM)
    smem = pl.BlockSpec(memory_space=pltpu.SMEM)
    return pl.pallas_call(
        move_kernel,
        out_shape=(part, part),
        in_specs=[smem, smem, vmem, vmem, vmem, vmem],
        out_specs=[vmem, vmem],
        scratch_shapes=[
            pltpu.VMEM((sources * slots, features), jnp.bfloat16),
            pltpu.VMEM((sources * slots, fines), jnp.bfloat16),
        ],
        name="move_sums",
        compiler_params=pltpu.CompilerParams(vmem_limit_bytes=ROOM),
    )(sharp, core, arrived, centres, norm, before)


def refresh_kernel(core_ref, mine_ref, other_ref, centres_ref, out_ref):
    copies, _, _ = out_ref.shape
    half, wide = mine_ref.shape
    features = wide - LANES
    total = mine_ref[...] + other_ref[...]
    mass = total[:, features:]
    core = core_ref[0]
    own = centres_ref[pl.ds(pl.multiple_of(core * half, half), half), :].astype(jnp.float32)
    scale = mass + 1.0
    for j in range(features // LANES):
        span = slice(j * LANES, (j + 1) * LANES)
        block = ((total[:, span] + own[:, span]) / scale).astype(jnp.bfloat16)
        for i in range(half // NOTE):
            at = (i * (features // LANES) + j) * NOTE
            piece = block[i * NOTE : (i + 1) * NOTE]
            for k in range(copies):
                out_ref[k, at : at + NOTE, :] = piece
    row = lax.broadcasted_iota(jnp.int32, (half, LANES), 0)
    lane = lax.broadcasted_iota(jnp.int32, (half, LANES), 1)
    flat = jnp.sum(jnp.where(row == lane, mass, 0.0), axis=0, keepdims=True)
    high = flat.astype(jnp.bfloat16).astype(jnp.float32)
    middle = (flat - high).astype(jnp.bfloat16).astype(jnp.float32)
    low = flat - high - middle
    line = lax.broadcasted_iota(jnp.int32, (NOTE, LANES), 0)
    note = jnp.where(line == 0, high, jnp.where(line == 1, middle, jnp.where(line == 2, low, 0.0)))
    note = note.astype(jnp.bfloat16)
    for k in range(copies):
        out_ref[k, half * features // LANES :, :] = note


def refresh(mine, other, centres, core, copies):
    half, wide = mine.shape
    fines, features = centres.shape
    whole = lambda *shape: pl.BlockSpec(shape, lambda: (0,) * len(shape))
    lines = half * features // LANES + NOTE
    return pl.pallas_call(
        refresh_kernel,
        out_shape=jax.ShapeDtypeStruct((copies, lines, LANES), jnp.bfloat16),
        in_specs=[
            pl.BlockSpec(memory_space=pltpu.SMEM),
            whole(half, wide),
            whole(half, wide),
            whole(fines, features),
        ],
        out_specs=whole(copies, lines, LANES),
        name="refresh",
        compiler_params=pltpu.CompilerParams(vmem_limit_bytes=ROOM),
    )(core, mine, other, centres)


def assemble_kernel(place_ref, near_ref, far_ref, out_hbm, mass_ref, out, sems):
    lists, share = mass_ref.shape
    _, fines, features = out.shape
    half = fines // 2
    tiles = features // LANES
    core, holder, offset = place_ref[0], place_ref[1], place_ref[2]

    def one(step, _):
        for ref, at in ((near_ref, core), (far_ref, 1 - core)):
            for i in range(half // NOTE):
                start = pl.multiple_of(at * half + i * NOTE, NOTE)
                for j in range(tiles):
                    line = (i * tiles + j) * NOTE
                    out[step, pl.ds(start, NOTE), j * LANES : (j + 1) * LANES] = ref[
                        step, line : line + NOTE, :
                    ]
        pltpu.make_async_copy(out.at[step], out_hbm.at[step], sems.at[step]).start()
        return 0

    lax.fori_loop(0, lists, one, 0)
    notes = half * tiles
    lane = lax.broadcasted_iota(jnp.int32, (1, LANES), 1)
    column = lax.broadcasted_iota(jnp.int32, (1, share), 1)
    for step in range(lists):
        near = near_ref[step, notes:, :].astype(jnp.float32)
        far = far_ref[step, notes:, :].astype(jnp.float32)
        note = jnp.where(holder == core, near, far)
        mass = (note[0:1] + note[1:2]) + note[2:3]
        result = jnp.zeros((1, share), jnp.float32)
        for k in range(share):
            value = jnp.sum(jnp.where(lane == offset + k, mass, 0.0), axis=1, keepdims=True)
            result = jnp.where(column == k, value, result)
        mass_ref[step : step + 1, :] = result
    for step in range(lists):
        pltpu.make_async_copy(out.at[step], out_hbm.at[step], sems.at[step]).wait()


def assemble(near, far, place, fines, features, share):
    lists, _, _ = near.shape
    vmem = pl.BlockSpec(memory_space=pltpu.VMEM)
    return pl.pallas_call(
        assemble_kernel,
        out_shape=(
            jax.ShapeDtypeStruct((lists, fines, features), jnp.bfloat16),
            jax.ShapeDtypeStruct((lists, share), jnp.float32),
        ),
        in_specs=[pl.BlockSpec(memory_space=pltpu.SMEM), vmem, vmem],
        out_specs=[pl.BlockSpec(memory_space=pl.ANY), vmem],
        scratch_shapes=[
            pltpu.VMEM((lists, fines, features), jnp.bfloat16),
            pltpu.SemaphoreType.DMA((lists,)),
        ],
        name="assemble",
        compiler_params=pltpu.CompilerParams(vmem_limit_bytes=ROOM),
    )(place, near, far)


def local(stay_rows, stay_count, moving_rows, new_list, centroids, sharpness):
    owners, columns, cores = (lax.axis_size(a) for a in ("owner", "y", "core"))
    lists_here, capacity, features = stay_rows.shape
    fine_count = centroids.shape[1]
    half = fine_count // cores
    share = fine_count // (columns * cores)
    y = lax.axis_index("y")
    core = lax.axis_index("core")

    outgoing = pack(moving_rows, new_list, owners * lists_here)
    arrived = lax.all_to_all(outgoing, ("owner", "y"), split_axis=0, concat_axis=0, tiled=True)

    dead = jnp.arange(capacity)[None, :, None] >= stay_count[:, :, None]
    first = jnp.arange(features)[None, None, :] == 0
    stay = jnp.where(dead & first, jnp.bfloat16(EMPTY), stay_rows)
    residents = []
    for by in range(columns):
        block = lax.dynamic_index_in_dim(stay, (y + by) & (columns - 1), 0, keepdims=False)
        residents.append(lax.ppermute(block, "y", shifted(columns, by)) if by else block)
    residents = jnp.concatenate(residents, axis=0)

    centres = lax.dynamic_index_in_dim(centroids, y, 0, keepdims=False)
    sharp = lax.dynamic_slice_in_dim(sharpness, y, 1, 0)
    norm = jnp.sum(jnp.square(centres.astype(jnp.float32)), axis=-1)[None, :]
    place = core.astype(jnp.int32)[None]
    before = stay_sums(residents, centres, norm, sharp)
    mine, theirs = move_sums(arrived, centres, norm, sharp, before, place)
    other = lax.ppermute(theirs, "core", shifted(cores, 1))
    copies = refresh(mine, other, centres, place, columns)
    near = lax.all_to_all(copies, "y", split_axis=0, concat_axis=0, tiled=True)
    far = lax.ppermute(near, "core", shifted(cores, 1))
    start = (y * cores + core) * share
    place = jnp.stack([core, start // half, start % half]).astype(jnp.int32)
    return assemble(near, far, place, fine_count, features, share)


def solution(mesh):
    split = Mesh(mesh.devices.reshape(mesh.devices.shape[0], -1, 2), ("owner", "y", "core"))
    rep = ("y", "core")
    in_specs = (
        P("owner", rep, None),
        P("owner", rep),
        P(("owner", "y", "core"), None),
        P(("owner", "y", "core")),
        P("owner", None, None),
        P("owner"),
    )
    out_specs = (P("owner", None, None), P("owner", rep))
    return jax.shard_map(
        local, mesh=split, in_specs=in_specs, out_specs=out_specs, check_vma=False
    )
```

```python
import math

import jax
import jax.numpy as jnp
from jax import lax
from jax.experimental import pallas as pl
from jax.experimental.pallas import tpu as pltpu
from jax.sharding import Mesh
from jax.sharding import PartitionSpec as P

SLOT_L = 2
EMPTY = 1024.0
LIMIT = 512.0
LANES = 128
NOTE = 16
ROOM = 24 * 1024 * 1024


def shifted(n, by):
    return [(i, (i + by) % n) for i in range(n)]


def pack_kernel(list_ref, rows_hbm, out_hbm, rows, out, sem, sems):
    lists, slots, features = out.shape
    blocks = sems.shape[0]
    block = lists // blocks
    many = block * slots
    count = rows.shape[0]
    fetch = pltpu.make_async_copy(rows_hbm, rows, sem)
    fetch.start()
    across = jnp.broadcast_to(list_ref[...], (count, count))
    down = jnp.transpose(across)
    row = lax.broadcasted_iota(jnp.int32, (count, count), 0)
    column = lax.broadcasted_iota(jnp.int32, (count, count), 1)
    earlier = jnp.where((across == down) & (row < column), 1.0, 0.0)
    slot = jnp.sum(earlier, axis=0, keepdims=True).astype(jnp.int32)
    position = list_ref[...] * slots + slot
    fetch.wait()

    def one(i, _):
        here = lax.broadcasted_iota(jnp.int32, (many, count), 0) + i * many
        pick = jnp.where(here == position, 1.0, 0.0)
        held = jnp.sum(pick, axis=1, keepdims=True)
        block_out = jnp.dot(
            pick.astype(jnp.bfloat16), rows[...], preferred_element_type=jnp.float32
        )
        lane = lax.broadcasted_iota(jnp.int32, (many, features), 1)
        block_out = jnp.where((lane == 0) & (held < 0.5), EMPTY, block_out)
        at = pl.ds(pl.multiple_of(i * block, block), block)
        out[at] = block_out.astype(jnp.bfloat16).reshape(block, slots, features)
        pltpu.make_async_copy(out.at[at], out_hbm.at[at], sems.at[i]).start()
        return 0

    lax.fori_loop(0, blocks, one, 0)
    for i in range(blocks):
        at = slice(i * block, (i + 1) * block)
        pltpu.make_async_copy(out.at[at], out_hbm.at[at], sems.at[i]).wait()


def pack(moving_rows, new_list, lists):
    count, features = moving_rows.shape
    blocks = 4
    return pl.pallas_call(
        pack_kernel,
        out_shape=jax.ShapeDtypeStruct((lists, SLOT_L, features), jnp.bfloat16),
        in_specs=[
            pl.BlockSpec(memory_space=pltpu.VMEM),
            pl.BlockSpec(memory_space=pl.ANY),
        ],
        out_specs=pl.BlockSpec(memory_space=pl.ANY),
        scratch_shapes=[
            pltpu.VMEM((count, features), jnp.bfloat16),
            pltpu.VMEM((lists, SLOT_L, features), jnp.bfloat16),
            pltpu.SemaphoreType.DMA,
            pltpu.SemaphoreType.DMA((blocks,)),
        ],
        name="pack",
    )(new_list[None, :], moving_rows)


DOWN = (((0,), (0,)), ((), ()))


def weights_of(members, centres, norm, sharp):
    features = members.shape[1]
    products = lax.dot_general(
        members, centres, (((1,), (1,)), ((), ())), preferred_element_type=jnp.float32
    )
    scores = sharp * (2.0 * products - norm) / math.sqrt(features)
    powers = jnp.exp(scores - jnp.max(scores, axis=1, keepdims=True))
    total = jnp.sum(powers, axis=1, keepdims=True)
    largest = jnp.max(members[:, :LANES].astype(jnp.float32), axis=1, keepdims=True)
    return (powers * jnp.where(largest < LIMIT, 1.0 / total, 0.0)).astype(jnp.bfloat16)


def weigh_block(members, centres, norm, sharp):
    weights = weights_of(members, centres, norm, sharp)
    numerator = lax.dot_general(weights, members, DOWN, preferred_element_type=jnp.float32)
    ones = jnp.ones((members.shape[0], LANES), jnp.bfloat16)
    mass = lax.dot_general(weights, ones, DOWN, preferred_element_type=jnp.float32)
    return numerator, mass


def stay_kernel(sharp_ref, members_ref, centres_ref, norm_ref, out_ref):
    features = centres_ref.shape[1]
    numerator, mass = weigh_block(members_ref[...], centres_ref[...], norm_ref[...], sharp_ref[0])

    @pl.when(pl.program_id(0) == 0)
    def _():
        out_ref[...] = jnp.zeros_like(out_ref)

    out_ref[:, :features] += numerator
    out_ref[:, features:] += mass


def stay_sums(members, centres, norm, sharp):
    rows, features = members.shape
    fines = centres.shape[0]
    steps = 2
    return pl.pallas_call(
        stay_kernel,
        out_shape=jax.ShapeDtypeStruct((fines, features + LANES), jnp.float32),
        grid=(steps,),
        in_specs=[
            pl.BlockSpec(memory_space=pltpu.SMEM),
            pl.BlockSpec((rows // steps, features), lambda i: (i, 0)),
            pl.BlockSpec((fines, features), lambda i: (0, 0)),
            pl.BlockSpec((1, fines), lambda i: (0, 0)),
        ],
        out_specs=pl.BlockSpec((fines, features + LANES), lambda i: (0, 0)),
        name="stay_sums",
        compiler_params=pltpu.CompilerParams(vmem_limit_bytes=ROOM),
    )(sharp, members, centres, norm)


def move_kernel(
    sharp_ref, core_ref, members_ref, centres_ref, norm_ref, before_ref, mine_ref, theirs_ref,
    members, weights,
):
    rows, features = members.shape
    half = mine_ref.shape[0]
    steps = 4
    block = rows // steps
    for i in range(steps):
        span = slice(i * block, (i + 1) * block)
        sources = slice(i * block // SLOT_L, (i + 1) * block // SLOT_L)
        part = members_ref[sources].reshape(block, features)
        members[span] = part
        weights[span] = weights_of(part, centres_ref[...], norm_ref[...], sharp_ref[0])

    first = core_ref[0] == 0

    def split(at, value):
        value = value + before_ref[:, at]
        mine_ref[:, at] = jnp.where(first, value[:half], value[half:])
        theirs_ref[:, at] = jnp.where(first, value[half:], value[:half])

    wide = 2 * LANES
    for j in range(features // wide):
        at = slice(j * wide, (j + 1) * wide)
        split(
            at,
            lax.dot_general(
                weights[...], members[:, at], DOWN, preferred_element_type=jnp.float32
            ),
        )
    ones = jnp.ones((rows, LANES), jnp.bfloat16)
    split(
        slice(features, features + LANES),
        lax.dot_general(weights[...], ones, DOWN, preferred_element_type=jnp.float32),
    )


def move_sums(arrived, centres, norm, sharp, before, core):
    sources, slots, features = arrived.shape
    fines = centres.shape[0]
    part = jax.ShapeDtypeStruct((fines // 2, features + LANES), jnp.float32)
    vmem = pl.BlockSpec(memory_space=pltpu.VMEM)
    smem = pl.BlockSpec(memory_space=pltpu.SMEM)
    return pl.pallas_call(
        move_kernel,
        out_shape=(part, part),
        in_specs=[smem, smem, vmem, vmem, vmem, vmem],
        out_specs=[vmem, vmem],
        scratch_shapes=[
            pltpu.VMEM((sources * slots, features), jnp.bfloat16),
            pltpu.VMEM((sources * slots, fines), jnp.bfloat16),
        ],
        name="move_sums",
        compiler_params=pltpu.CompilerParams(vmem_limit_bytes=ROOM),
    )(sharp, core, arrived, centres, norm, before)


def refresh_kernel(core_ref, mine_ref, other_ref, centres_ref, out_ref):
    copies, _, _ = out_ref.shape
    half, wide = mine_ref.shape
    features = wide - LANES
    total = mine_ref[...] + other_ref[...]
    mass = total[:, features:]
    core = core_ref[0]
    own = centres_ref[pl.ds(pl.multiple_of(core * half, half), half), :].astype(jnp.float32)
    scale = mass + 1.0
    for j in range(features // LANES):
        span = slice(j * LANES, (j + 1) * LANES)
        block = ((total[:, span] + own[:, span]) / scale).astype(jnp.bfloat16)
        for i in range(half // NOTE):
            at = (i * (features // LANES) + j) * NOTE
            piece = block[i * NOTE : (i + 1) * NOTE]
            for k in range(copies):
                out_ref[k, at : at + NOTE, :] = piece
    row = lax.broadcasted_iota(jnp.int32, (half, LANES), 0)
    lane = lax.broadcasted_iota(jnp.int32, (half, LANES), 1)
    flat = jnp.sum(jnp.where(row == lane, mass, 0.0), axis=0, keepdims=True)
    high = flat.astype(jnp.bfloat16).astype(jnp.float32)
    middle = (flat - high).astype(jnp.bfloat16).astype(jnp.float32)
    low = flat - high - middle
    line = lax.broadcasted_iota(jnp.int32, (NOTE, LANES), 0)
    note = jnp.where(line == 0, high, jnp.where(line == 1, middle, jnp.where(line == 2, low, 0.0)))
    note = note.astype(jnp.bfloat16)
    for k in range(copies):
        out_ref[k, half * features // LANES :, :] = note


def refresh(mine, other, centres, core, copies):
    half, wide = mine.shape
    fines, features = centres.shape
    whole = lambda *shape: pl.BlockSpec(shape, lambda: (0,) * len(shape))
    lines = half * features // LANES + NOTE
    return pl.pallas_call(
        refresh_kernel,
        out_shape=jax.ShapeDtypeStruct((copies, lines, LANES), jnp.bfloat16),
        in_specs=[
            pl.BlockSpec(memory_space=pltpu.SMEM),
            whole(half, wide),
            whole(half, wide),
            whole(fines, features),
        ],
        out_specs=whole(copies, lines, LANES),
        name="refresh",
        compiler_params=pltpu.CompilerParams(vmem_limit_bytes=ROOM),
    )(core, mine, other, centres)


def place_half(ref, at, out_hbm, held, sems):
    lists, half, features = held.shape
    tiles = features // LANES
    rows = pl.ds(pl.multiple_of(at * half, half), half)

    def one(step, _):
        for i in range(half // NOTE):
            for j in range(tiles):
                line = (i * tiles + j) * NOTE
                held[step, i * NOTE : (i + 1) * NOTE, j * LANES : (j + 1) * LANES] = ref[
                    step, line : line + NOTE, :
                ]
        pltpu.make_async_copy(held.at[step], out_hbm.at[step, rows], sems.at[step]).start()
        return 0

    lax.fori_loop(0, lists, one, 0)


def wait_half(at, out_hbm, held, sems):
    lists, half, _ = held.shape
    rows = pl.ds(pl.multiple_of(at * half, half), half)
    for step in range(lists):
        pltpu.make_async_copy(held.at[step], out_hbm.at[step, rows], sems.at[step]).wait()


def near_kernel(place_ref, near_ref, out_hbm, held, sems):
    place_half(near_ref, place_ref[0], out_hbm, held, sems)
    wait_half(place_ref[0], out_hbm, held, sems)


def far_kernel(place_ref, near_ref, far_ref, begun_hbm, out_hbm, mass_ref, held, sems):
    del begun_hbm
    lists, share = mass_ref.shape
    notes = near_ref.shape[1] - NOTE
    core, holder, offset = place_ref[0], place_ref[1], place_ref[2]
    place_half(far_ref, 1 - core, out_hbm, held, sems)
    lane = lax.broadcasted_iota(jnp.int32, (1, LANES), 1)
    column = lax.broadcasted_iota(jnp.int32, (1, share), 1)
    for step in range(lists):
        near = near_ref[step, notes:, :].astype(jnp.float32)
        far = far_ref[step, notes:, :].astype(jnp.float32)
        note = jnp.where(holder == core, near, far)
        mass = (note[0:1] + note[1:2]) + note[2:3]
        result = jnp.zeros((1, share), jnp.float32)
        for k in range(share):
            value = jnp.sum(jnp.where(lane == offset + k, mass, 0.0), axis=1, keepdims=True)
            result = jnp.where(column == k, value, result)
        mass_ref[step : step + 1, :] = result
    wait_half(1 - core, out_hbm, held, sems)


def assemble_near(near, place, fines, features):
    lists, _, _ = near.shape
    return pl.pallas_call(
        near_kernel,
        out_shape=jax.ShapeDtypeStruct((lists, fines, features), jnp.bfloat16),
        in_specs=[pl.BlockSpec(memory_space=pltpu.SMEM), pl.BlockSpec(memory_space=pltpu.VMEM)],
        out_specs=pl.BlockSpec(memory_space=pl.ANY),
        scratch_shapes=[
            pltpu.VMEM((lists, fines // 2, features), jnp.bfloat16),
            pltpu.SemaphoreType.DMA((lists,)),
        ],
        name="assemble_near",
        cost_estimate=pl.CostEstimate(
            flops=0, bytes_accessed=lists * fines * features * 2, transcendentals=0
        ),
        compiler_params=pltpu.CompilerParams(vmem_limit_bytes=ROOM),
    )(place, near)


def assemble_far(near, far, begun, place, share):
    lists, fines, features = begun.shape
    vmem = pl.BlockSpec(memory_space=pltpu.VMEM)
    hbm = pl.BlockSpec(memory_space=pl.ANY)
    return pl.pallas_call(
        far_kernel,
        out_shape=(
            jax.ShapeDtypeStruct(begun.shape, begun.dtype),
            jax.ShapeDtypeStruct((lists, share), jnp.float32),
        ),
        in_specs=[pl.BlockSpec(memory_space=pltpu.SMEM), vmem, vmem, hbm],
        out_specs=[hbm, vmem],
        scratch_shapes=[
            pltpu.VMEM((lists, fines // 2, features), jnp.bfloat16),
            pltpu.SemaphoreType.DMA((lists,)),
        ],
        input_output_aliases={3: 0},
        name="assemble_far",
        compiler_params=pltpu.CompilerParams(vmem_limit_bytes=ROOM),
    )(place, near, far, begun)


def local(stay_rows, stay_count, moving_rows, new_list, centroids, sharpness):
    owners, columns, cores = (lax.axis_size(a) for a in ("owner", "y", "core"))
    lists_here, capacity, features = stay_rows.shape
    fine_count = centroids.shape[1]
    half = fine_count // cores
    share = fine_count // (columns * cores)
    y = lax.axis_index("y")
    core = lax.axis_index("core")

    outgoing = pack(moving_rows, new_list, owners * lists_here)
    arrived = lax.all_to_all(outgoing, ("owner", "y"), split_axis=0, concat_axis=0, tiled=True)

    dead = jnp.arange(capacity)[None, :, None] >= stay_count[:, :, None]
    first = jnp.arange(features)[None, None, :] == 0
    stay = jnp.where(dead & first, jnp.bfloat16(EMPTY), stay_rows)
    residents = []
    for by in range(columns):
        block = lax.dynamic_index_in_dim(stay, (y + by) & (columns - 1), 0, keepdims=False)
        residents.append(lax.ppermute(block, "y", shifted(columns, by)) if by else block)
    residents = jnp.concatenate(residents, axis=0)

    centres = lax.dynamic_index_in_dim(centroids, y, 0, keepdims=False)
    sharp = lax.dynamic_slice_in_dim(sharpness, y, 1, 0)
    norm = jnp.sum(jnp.square(centres.astype(jnp.float32)), axis=-1)[None, :]
    place = core.astype(jnp.int32)[None]
    before = stay_sums(residents, centres, norm, sharp)
    mine, theirs = move_sums(arrived, centres, norm, sharp, before, place)
    other = lax.ppermute(theirs, "core", shifted(cores, 1))
    copies = refresh(mine, other, centres, place, columns)
    near = lax.all_to_all(copies, "y", split_axis=0, concat_axis=0, tiled=True)
    far = lax.ppermute(near, "core", shifted(cores, 1))
    start = (y * cores + core) * share
    place = jnp.stack([core, start // half, start % half]).astype(jnp.int32)
    begun = assemble_near(near, place, fine_count, features)
    return assemble_far(near, far, begun, place, share)


def solution(mesh):
    split = Mesh(mesh.devices.reshape(mesh.devices.shape[0], -1, 2), ("owner", "y", "core"))
    rep = ("y", "core")
    in_specs = (
        P("owner", rep, None),
        P("owner", rep),
        P(("owner", "y", "core"), None),
        P(("owner", "y", "core")),
        P("owner", None, None),
        P("owner"),
    )
    out_specs = (P("owner", None, None), P("owner", rep))
    return jax.shard_map(
        local, mesh=split, in_specs=in_specs, out_specs=out_specs, check_vma=False
    )
```

```python
import math

import jax
import jax.numpy as jnp
from jax import lax
from jax.experimental import pallas as pl
from jax.experimental.pallas import tpu as pltpu
from jax.sharding import Mesh
from jax.sharding import PartitionSpec as P

SLOT_L = 2
EMPTY = 1024.0
LIMIT = 512.0
LANES = 128
TILE = 16
NOTE = 8
ROOM = 24 * 1024 * 1024


def shifted(n, by):
    return [(i, (i + by) % n) for i in range(n)]


def pack_kernel(list_ref, rows_hbm, out_hbm, rows, out, sem, sems):
    lists, slots, features = out.shape
    blocks = sems.shape[0]
    block = lists // blocks
    many = block * slots
    count = rows.shape[0]
    fetch = pltpu.make_async_copy(rows_hbm, rows, sem)
    fetch.start()
    across = jnp.broadcast_to(list_ref[...], (count, count))
    down = jnp.transpose(across)
    row = lax.broadcasted_iota(jnp.int32, (count, count), 0)
    column = lax.broadcasted_iota(jnp.int32, (count, count), 1)
    earlier = jnp.where((across == down) & (row < column), 1.0, 0.0)
    slot = jnp.sum(earlier, axis=0, keepdims=True).astype(jnp.int32)
    position = list_ref[...] * slots + slot
    fetch.wait()

    def one(i, _):
        here = lax.broadcasted_iota(jnp.int32, (many, count), 0) + i * many
        pick = jnp.where(here == position, 1.0, 0.0)
        held = jnp.sum(pick, axis=1, keepdims=True)
        block_out = jnp.dot(
            pick.astype(jnp.bfloat16), rows[...], preferred_element_type=jnp.float32
        )
        lane = lax.broadcasted_iota(jnp.int32, (many, features), 1)
        block_out = jnp.where((lane == 0) & (held < 0.5), EMPTY, block_out)
        at = pl.ds(pl.multiple_of(i * block, block), block)
        out[at] = block_out.astype(jnp.bfloat16).reshape(block, slots, features)
        pltpu.make_async_copy(out.at[at], out_hbm.at[at], sems.at[i]).start()
        return 0

    lax.fori_loop(0, blocks, one, 0)
    for i in range(blocks):
        at = slice(i * block, (i + 1) * block)
        pltpu.make_async_copy(out.at[at], out_hbm.at[at], sems.at[i]).wait()


def pack(moving_rows, new_list, lists):
    count, features = moving_rows.shape
    blocks = 4
    return pl.pallas_call(
        pack_kernel,
        out_shape=jax.ShapeDtypeStruct((lists, SLOT_L, features), jnp.bfloat16),
        in_specs=[
            pl.BlockSpec(memory_space=pltpu.VMEM),
            pl.BlockSpec(memory_space=pl.ANY),
        ],
        out_specs=pl.BlockSpec(memory_space=pl.ANY),
        scratch_shapes=[
            pltpu.VMEM((count, features), jnp.bfloat16),
            pltpu.VMEM((lists, SLOT_L, features), jnp.bfloat16),
            pltpu.SemaphoreType.DMA,
            pltpu.SemaphoreType.DMA((blocks,)),
        ],
        name="pack",
    )(new_list[None, :], moving_rows)


DOWN = (((0,), (0,)), ((), ()))


def weights_of(members, centres, norm, sharp):
    features = members.shape[1]
    products = lax.dot_general(
        members, centres, (((1,), (1,)), ((), ())), preferred_element_type=jnp.float32
    )
    scores = sharp * (2.0 * products - norm) / math.sqrt(features)
    powers = jnp.exp(scores - jnp.max(scores, axis=1, keepdims=True))
    total = jnp.sum(powers, axis=1, keepdims=True)
    largest = jnp.max(members[:, :LANES].astype(jnp.float32), axis=1, keepdims=True)
    return (powers * jnp.where(largest < LIMIT, 1.0 / total, 0.0)).astype(jnp.bfloat16)


def weigh_block(members, centres, norm, sharp):
    weights = weights_of(members, centres, norm, sharp)
    numerator = lax.dot_general(weights, members, DOWN, preferred_element_type=jnp.float32)
    ones = jnp.ones((members.shape[0], LANES), jnp.bfloat16)
    mass = lax.dot_general(weights, ones, DOWN, preferred_element_type=jnp.float32)
    return numerator, mass


def stay_kernel(sharp_ref, members_ref, centres_ref, norm_ref, out_ref):
    features = centres_ref.shape[1]
    numerator, mass = weigh_block(members_ref[...], centres_ref[...], norm_ref[...], sharp_ref[0])

    @pl.when(pl.program_id(0) == 0)
    def _():
        out_ref[...] = jnp.zeros_like(out_ref)

    out_ref[:, :features] += numerator
    out_ref[:, features:] += mass


def stay_sums(members, centres, norm, sharp):
    rows, features = members.shape
    fines = centres.shape[0]
    steps = 2
    return pl.pallas_call(
        stay_kernel,
        out_shape=jax.ShapeDtypeStruct((fines, features + LANES), jnp.float32),
        grid=(steps,),
        in_specs=[
            pl.BlockSpec(memory_space=pltpu.SMEM),
            pl.BlockSpec((rows // steps, features), lambda i: (i, 0)),
            pl.BlockSpec((fines, features), lambda i: (0, 0)),
            pl.BlockSpec((1, fines), lambda i: (0, 0)),
        ],
        out_specs=pl.BlockSpec((fines, features + LANES), lambda i: (0, 0)),
        name="stay_sums",
        compiler_params=pltpu.CompilerParams(vmem_limit_bytes=ROOM),
    )(sharp, members, centres, norm)


def move_kernel(
    sharp_ref, core_ref, members_ref, centres_ref, norm_ref, before_ref, mine_ref, theirs_ref,
    members, weights,
):
    rows, features = members.shape
    half = mine_ref.shape[0]
    steps = 4
    block = rows // steps
    for i in range(steps):
        span = slice(i * block, (i + 1) * block)
        sources = slice(i * block // SLOT_L, (i + 1) * block // SLOT_L)
        part = members_ref[sources].reshape(block, features)
        members[span] = part
        weights[span] = weights_of(part, centres_ref[...], norm_ref[...], sharp_ref[0])

    first = core_ref[0] == 0

    def split(at, value):
        value = value + before_ref[:, at]
        mine_ref[:, at] = jnp.where(first, value[:half], value[half:])
        theirs_ref[:, at] = jnp.where(first, value[half:], value[:half])

    wide = 2 * LANES
    for j in range(features // wide):
        at = slice(j * wide, (j + 1) * wide)
        split(
            at,
            lax.dot_general(
                weights[...], members[:, at], DOWN, preferred_element_type=jnp.float32
            ),
        )
    ones = jnp.ones((rows, LANES), jnp.bfloat16)
    split(
        slice(features, features + LANES),
        lax.dot_general(weights[...], ones, DOWN, preferred_element_type=jnp.float32),
    )


def move_sums(arrived, centres, norm, sharp, before, core):
    sources, slots, features = arrived.shape
    fines = centres.shape[0]
    part = jax.ShapeDtypeStruct((fines // 2, features + LANES), jnp.float32)
    vmem = pl.BlockSpec(memory_space=pltpu.VMEM)
    smem = pl.BlockSpec(memory_space=pltpu.SMEM)
    return pl.pallas_call(
        move_kernel,
        out_shape=(part, part),
        in_specs=[smem, smem, vmem, vmem, vmem, vmem],
        out_specs=[vmem, vmem],
        scratch_shapes=[
            pltpu.VMEM((sources * slots, features), jnp.bfloat16),
            pltpu.VMEM((sources * slots, fines), jnp.bfloat16),
        ],
        name="move_sums",
        compiler_params=pltpu.CompilerParams(vmem_limit_bytes=ROOM),
    )(sharp, core, arrived, centres, norm, before)


def refresh_kernel(core_ref, mine_ref, other_ref, centres_ref, out_ref):
    copies, _, _ = out_ref.shape
    half, wide = mine_ref.shape
    features = wide - LANES
    total = mine_ref[...] + other_ref[...]
    mass = total[:, features:]
    core = core_ref[0]
    own = centres_ref[pl.ds(pl.multiple_of(core * half, half), half), :].astype(jnp.float32)
    scale = mass + 1.0
    for j in range(features // LANES):
        span = slice(j * LANES, (j + 1) * LANES)
        block = ((total[:, span] + own[:, span]) / scale).astype(jnp.bfloat16)
        for i in range(half // TILE):
            at = (i * (features // LANES) + j) * TILE
            piece = block[i * TILE : (i + 1) * TILE]
            for k in range(copies):
                out_ref[k, at : at + TILE, :] = piece
    row = lax.broadcasted_iota(jnp.int32, (half, LANES), 0)
    lane = lax.broadcasted_iota(jnp.int32, (half, LANES), 1)
    flat = jnp.sum(jnp.where(row == lane, mass, 0.0), axis=0, keepdims=True)
    high = flat.astype(jnp.bfloat16).astype(jnp.float32)
    middle = (flat - high).astype(jnp.bfloat16).astype(jnp.float32)
    low = flat - high - middle
    line = lax.broadcasted_iota(jnp.int32, (NOTE, LANES), 0)
    note = jnp.where(line == 0, high, jnp.where(line == 1, middle, jnp.where(line == 2, low, 0.0)))
    note = note.astype(jnp.bfloat16)
    for k in range(copies):
        out_ref[k, half * features // LANES :, :] = note


def refresh(mine, other, centres, core, copies):
    half, wide = mine.shape
    fines, features = centres.shape
    whole = lambda *shape: pl.BlockSpec(shape, lambda: (0,) * len(shape))
    lines = half * features // LANES + NOTE
    return pl.pallas_call(
        refresh_kernel,
        out_shape=jax.ShapeDtypeStruct((copies, lines, LANES), jnp.bfloat16),
        in_specs=[
            pl.BlockSpec(memory_space=pltpu.SMEM),
            whole(half, wide),
            whole(half, wide),
            whole(fines, features),
        ],
        out_specs=whole(copies, lines, LANES),
        name="refresh",
        compiler_params=pltpu.CompilerParams(vmem_limit_bytes=ROOM),
    )(core, mine, other, centres)


def place_half(ref, at, out_hbm, held, sems):
    lists, half, features = held.shape
    tiles = features // LANES
    rows = pl.ds(pl.multiple_of(at * half, half), half)

    def one(step, _):
        for i in range(half // TILE):
            for j in range(tiles):
                line = (i * tiles + j) * TILE
                held[step, i * TILE : (i + 1) * TILE, j * LANES : (j + 1) * LANES] = ref[
                    step, line : line + TILE, :
                ]
        pltpu.make_async_copy(held.at[step], out_hbm.at[step, rows], sems.at[step]).start()
        return 0

    lax.fori_loop(0, lists, one, 0)


def wait_half(at, out_hbm, held, sems):
    lists, half, _ = held.shape
    rows = pl.ds(pl.multiple_of(at * half, half), half)
    for step in range(lists):
        pltpu.make_async_copy(held.at[step], out_hbm.at[step, rows], sems.at[step]).wait()


def near_kernel(place_ref, near_ref, out_hbm, held, sems):
    place_half(near_ref, place_ref[0], out_hbm, held, sems)
    wait_half(place_ref[0], out_hbm, held, sems)


def far_kernel(place_ref, near_ref, far_ref, begun_hbm, out_hbm, mass_ref, held, sems):
    del begun_hbm
    lists, share = mass_ref.shape
    notes = near_ref.shape[1] - NOTE
    core, holder, offset = place_ref[0], place_ref[1], place_ref[2]
    place_half(far_ref, 1 - core, out_hbm, held, sems)
    masses = []
    for step in range(lists):
        near = near_ref[step, notes:, :].astype(jnp.float32)
        far = far_ref[step, notes:, :].astype(jnp.float32)
        note = jnp.where(holder == core, near, far)
        masses.append((note[0:1] + note[1:2]) + note[2:3])
    masses = jnp.concatenate(masses, axis=0)
    lane = lax.broadcasted_iota(jnp.int32, (lists, LANES), 1)
    column = lax.broadcasted_iota(jnp.int32, (lists, share), 1)
    result = jnp.zeros((lists, share), jnp.float32)
    for k in range(share):
        value = jnp.sum(jnp.where(lane == offset + k, masses, 0.0), axis=1, keepdims=True)
        result = jnp.where(column == k, value, result)
    mass_ref[...] = result
    wait_half(1 - core, out_hbm, held, sems)


def assemble_near(near, place, fines, features):
    lists, _, _ = near.shape
    return pl.pallas_call(
        near_kernel,
        out_shape=jax.ShapeDtypeStruct((lists, fines, features), jnp.bfloat16),
        in_specs=[pl.BlockSpec(memory_space=pltpu.SMEM), pl.BlockSpec(memory_space=pltpu.VMEM)],
        out_specs=pl.BlockSpec(memory_space=pl.ANY),
        scratch_shapes=[
            pltpu.VMEM((lists, fines // 2, features), jnp.bfloat16),
            pltpu.SemaphoreType.DMA((lists,)),
        ],
        name="assemble_near",
        cost_estimate=pl.CostEstimate(
            flops=0, bytes_accessed=lists * fines * features * 2, transcendentals=0
        ),
        compiler_params=pltpu.CompilerParams(vmem_limit_bytes=ROOM),
    )(place, near)


def assemble_far(near, far, begun, place, share):
    lists, fines, features = begun.shape
    vmem = pl.BlockSpec(memory_space=pltpu.VMEM)
    hbm = pl.BlockSpec(memory_space=pl.ANY)
    return pl.pallas_call(
        far_kernel,
        out_shape=(
            jax.ShapeDtypeStruct(begun.shape, begun.dtype),
            jax.ShapeDtypeStruct((lists, share), jnp.float32),
        ),
        in_specs=[pl.BlockSpec(memory_space=pltpu.SMEM), vmem, vmem, hbm],
        out_specs=[hbm, vmem],
        scratch_shapes=[
            pltpu.VMEM((lists, fines // 2, features), jnp.bfloat16),
            pltpu.SemaphoreType.DMA((lists,)),
        ],
        input_output_aliases={3: 0},
        name="assemble_far",
        compiler_params=pltpu.CompilerParams(vmem_limit_bytes=ROOM),
    )(place, near, far, begun)


def local(stay_rows, stay_count, moving_rows, new_list, centroids, sharpness):
    owners, columns, cores = (lax.axis_size(a) for a in ("owner", "y", "core"))
    lists_here, capacity, features = stay_rows.shape
    fine_count = centroids.shape[1]
    half = fine_count // cores
    share = fine_count // (columns * cores)
    y = lax.axis_index("y")
    core = lax.axis_index("core")

    outgoing = pack(moving_rows, new_list, owners * lists_here)
    arrived = lax.all_to_all(outgoing, ("owner", "y"), split_axis=0, concat_axis=0, tiled=True)

    dead = jnp.arange(capacity)[None, :, None] >= stay_count[:, :, None]
    first = jnp.arange(features)[None, None, :] == 0
    stay = jnp.where(dead & first, jnp.bfloat16(EMPTY), stay_rows)
    residents = []
    for by in range(columns):
        block = lax.dynamic_index_in_dim(stay, (y + by) & (columns - 1), 0, keepdims=False)
        residents.append(lax.ppermute(block, "y", shifted(columns, by)) if by else block)
    residents = jnp.concatenate(residents, axis=0)

    centres = lax.dynamic_index_in_dim(centroids, y, 0, keepdims=False)
    sharp = lax.dynamic_slice_in_dim(sharpness, y, 1, 0)
    norm = jnp.sum(jnp.square(centres.astype(jnp.float32)), axis=-1)[None, :]
    place = core.astype(jnp.int32)[None]
    before = stay_sums(residents, centres, norm, sharp)
    mine, theirs = move_sums(arrived, centres, norm, sharp, before, place)
    other = lax.ppermute(theirs, "core", shifted(cores, 1))
    copies = refresh(mine, other, centres, place, columns)
    near = lax.all_to_all(copies, "y", split_axis=0, concat_axis=0, tiled=True)
    far = lax.ppermute(near, "core", shifted(cores, 1))
    start = (y * cores + core) * share
    place = jnp.stack([core, start // half, start % half]).astype(jnp.int32)
    begun = assemble_near(near, place, fine_count, features)
    return assemble_far(near, far, begun, place, share)


def solution(mesh):
    split = Mesh(mesh.devices.reshape(mesh.devices.shape[0], -1, 2), ("owner", "y", "core"))
    rep = ("y", "core")
    in_specs = (
        P("owner", rep, None),
        P("owner", rep),
        P(("owner", "y", "core"), None),
        P(("owner", "y", "core")),
        P("owner", None, None),
        P("owner"),
    )
    out_specs = (P("owner", None, None), P("owner", rep))
    return jax.shard_map(
        local, mesh=split, in_specs=in_specs, out_specs=out_specs, check_vma=False
    )
```
